128 devices in a mesh: row: 32 (over x, z, y_lo), loop: 4 (over y_hi, core).
Axes of the slice: x: 4, y: 4 (y_hi: 2, y_lo: 2; y = y_hi * 2 + y_lo), z: 4, core: 2. Of those that a mesh axis runs over, the one named last changes fastest.
Arguments:
- pair: bfloat16 [768, 768, 128], P('row', 'loop'), may hold values from -6 to 6
- ln_in_gain: float32 [128], replicated, may hold values from 0.1 to 1.9
- ln_in_bias: float32 [128], replicated, may hold values from -3 to 3
- w_proj: bfloat16 [128, 512], replicated, may hold values from -0.5 to 0.5
- w_gate: bfloat16 [128, 128], replicated, may hold values from -0.5 to 0.5
- ln_out_gain: float32 [128], replicated, may hold values from 0.1 to 1.9
- ln_out_bias: float32 [128], replicated, may hold values from -3 to 3
- w_out: bfloat16 [128, 128], replicated, may hold values from -0.5 to 0.5
Outputs:
- update: bfloat16 [768, 768, 128], P('row', 'loop')
The draws below stay inside these ranges and needn't reach their ends.
All inputs are finite; a program needn't handle non-finite values.
Results may differ from the reference program's by a relative error of at most 0.0055.
Values may be sent and summed in bfloat16 or wider, within the bound.
A program may use at most 192 MiB of HBM per device.

```python
import jax
import jax.numpy as jnp
from jax import lax

C = 128
H = 128
ROWS_DEV = 24
N = 768


def level_of(rng, dims, split, smallest, largest):
    def one(dim, parts):
        heights = jax.random.uniform(jax.random.fold_in(jax.random.fold_in(rng, 6), dim), (parts,), jnp.float32, smallest / len(split), largest / len(split))
        return jnp.repeat(jnp.exp(heights), dims[dim] // parts).reshape((-1,) + (1,) * (len(dims) - dim - 1))

    level = one(*split[0])
    for cut in split[1:]:
        level = level * one(*cut)
    return level


def gaussian(rng, dims, scale, reach, split=(), dtype=jnp.bfloat16):
    values = jax.random.normal(rng, dims, jnp.float32) * scale
    if len(split) > 0:
        values = level_of(rng, dims, split, -0.22, 0.18) * values
    return jnp.clip(values, min=-reach, max=reach).astype(dtype)


def setup_inputs(seed: int = 0) -> dict:
    key_of = jax.random.split(jax.random.key(seed), 9)
    return {
        "pair": gaussian(key_of[0], (N, N, C), 1.0, 6.0, ((0, 32), (1, 4))),
        "ln_in_gain": jnp.clip(1.0 + 0.18 * jax.random.normal(key_of[1], (C,), jnp.float32), 0.1, 1.9),
        "ln_in_bias": gaussian(key_of[2], (C,), 0.5, 3.0, (), jnp.float32),
        "w_proj": gaussian(key_of[3], (C, 4 * H), C ** -0.5, 0.5),
        "w_gate": gaussian(key_of[4], (C, C), C ** -0.5, 0.5),
        "ln_out_gain": jnp.clip(1.0 + 0.18 * jax.random.normal(key_of[5], (H,), jnp.float32), 0.1, 1.9),
        "ln_out_bias": gaussian(key_of[6], (H,), 0.5, 3.0, (), jnp.float32),
        "w_out": gaussian(key_of[7], (H, C), H ** -0.5, 0.5),
    }


epsilon = 1e-05

def layer_norm(values, gain, bias):
    values = values.astype(jnp.float32)
    center = values - lax.optimization_barrier(jnp.mean(values, axis=-1, keepdims=True))
    spread = lax.optimization_barrier(jnp.mean(center * center, axis=-1, keepdims=True))
    return center * lax.rsqrt(spread + epsilon) * gain + bias

def reference(pair, ln_in_gain, ln_in_bias, w_proj, w_gate, ln_out_gain, ln_out_bias, w_out):
    normed = layer_norm(pair, ln_in_gain, ln_in_bias).astype(jnp.bfloat16)
    projected = jnp.dot(normed.reshape(N * N, C), w_proj, preferred_element_type=jnp.float32)
    projected = projected.reshape(N, N, 4 * H)
    left = (jax.nn.sigmoid(projected[:, :, :H]) * projected[:, :, H:2 * H]).astype(jnp.bfloat16)
    right = (jax.nn.sigmoid(projected[:, :, 2 * H:3 * H]) * projected[:, :, 3 * H:]).astype(jnp.bfloat16)
    right_wide = right.astype(jnp.float32)

    def one_block(first):
        left_part = lax.dynamic_slice_in_dim(left, first, ROWS_DEV, 1).astype(jnp.float32)
        triangle = jnp.einsum('kic,kjc->ijc', left_part, right_wide)
        mixed = layer_norm(triangle, ln_out_gain, ln_out_bias).astype(jnp.bfloat16)
        outgoing = jnp.dot(mixed.reshape(ROWS_DEV * N, H), w_out, preferred_element_type=jnp.float32)
        normed_part = lax.dynamic_slice_in_dim(normed, first, ROWS_DEV, 0).reshape(ROWS_DEV * N, C)
        gating = jax.nn.sigmoid(jnp.dot(normed_part, w_gate, preferred_element_type=jnp.float32))
        return (gating * outgoing).astype(jnp.bfloat16).reshape(ROWS_DEV, N, C)
    starts = (jnp.arange(N // ROWS_DEV) * ROWS_DEV).astype(jnp.int32)
    blocks = lax.map(one_block, starts)
    return blocks.reshape(N, N, C)
```

```python
import functools

import jax
import jax.numpy as jnp
from jax import lax
from jax.experimental import pallas as pl
from jax.experimental.pallas import tpu as pltpu
from jax.sharding import PartitionSpec as P

epsilon = 1e-05
MESH = pl.DeviceIdType.MESH
f32 = jnp.float32
bf16 = jnp.bfloat16
CHIPS = 64
NT = (((1,), (1,)), ((), ()))
TN = (((0,), (0,)), ((), ()))


def normalize(values, gain, bias):
    center = values - jnp.mean(values, axis=-1, keepdims=True)
    spread = jnp.mean(center * center, axis=-1, keepdims=True)
    return center * lax.rsqrt(spread + epsilon) * gain + bias


def project_kernel(pair_ref, gain_ref, bias_ref, w_ref, wg_ref, left_ref, right_ref, gate_ref,
                   wide, tall, major_l, major_r, normed):
    @pl.when(pl.program_id(0) == 0)
    def _():
        flipped = w_ref[...].astype(f32).T.astype(bf16)
        wide[...] = flipped
        for kind in range(4):
            rows = pl.ds(64 * kind, 64)
            tall[rows, 0:128] = flipped[128 * kind:128 * kind + 64]
            tall[rows, 128:256] = flipped[128 * kind + 64:128 * kind + 128]

    gain = gain_ref[...]
    bias = bias_ref[...]
    for k in range(8):
        values = normalize(pair_ref[k].astype(f32), gain, bias).astype(bf16)
        normed[k] = values
        head = values[0:128]
        rest = values[128:192]
        zero = jnp.zeros_like(rest)
        both = jnp.concatenate(
            [jnp.concatenate([rest, zero], axis=1), jnp.concatenate([zero, rest], axis=1)], axis=0
        )
        a = lax.dot_general(wide[...], head, NT, preferred_element_type=f32)
        b = lax.dot_general(tall[...], both, NT, preferred_element_type=f32)
        rows = pl.ds(64 * k, 64)
        for major, at in ((major_l, 0), (major_r, 1)):
            full = jax.nn.sigmoid(a[256 * at:256 * at + 128]) * a[256 * at + 128:256 * at + 256]
            part = jax.nn.sigmoid(b[128 * at:128 * at + 64]) * b[128 * at + 64:128 * at + 128]
            major[0, rows] = full[0:64]
            major[1, rows] = part
            major[2, rows] = full[64:128]
        gate = jnp.dot(values, wg_ref[...], preferred_element_type=f32)
        gate_ref[k] = jax.nn.sigmoid(gate)
    for c in range(CHIPS):
        for part in range(3):
            lanes = pl.ds(128 * part, 128)
            picked = pl.ds(c, 8, stride=64)
            left_ref[c, 0, :, lanes] = major_l[part, picked, :].astype(bf16)
            right_ref[c, 0, :, lanes] = major_r[part, picked, :].astype(bf16)


def project(pair, gain, bias, w_proj, w_gate):
    whole = lambda shape: pl.BlockSpec(shape, lambda i: (0,) * len(shape))
    message = jax.ShapeDtypeStruct((CHIPS, 3, 8, 384), bf16)
    return pl.pallas_call(
        project_kernel,
        name="project",
        grid=(3,),
        out_shape=(message, message, jax.ShapeDtypeStruct((24, 192, 128), f32)),
        in_specs=[
            pl.BlockSpec((8, 192, 128), lambda i: (i, 0, 0)),
            whole((1, 128)), whole((1, 128)), whole((128, 512)), whole((128, 128)),
        ],
        out_specs=(
            pl.BlockSpec((CHIPS, 1, 8, 384), lambda i: (0, i, 0, 0)),
            pl.BlockSpec((CHIPS, 1, 8, 384), lambda i: (0, i, 0, 0)),
            pl.BlockSpec((8, 192, 128), lambda i: (i, 0, 0)),
        ),
        scratch_shapes=[
            pltpu.VMEM((512, 128), bf16),
            pltpu.VMEM((256, 256), bf16),
            pltpu.VMEM((3, 512, 128), f32),
            pltpu.VMEM((3, 512, 128), f32),
            pltpu.VMEM((8, 192, 128), bf16),
        ],
        compiler_params=pltpu.CompilerParams(dimension_semantics=("arbitrary",)),
    )(pair, gain, bias, w_proj, w_gate)


def exchange_kernel(left_ref, right_ref, out_ref, own, other, right, flipped, outgoing,
                    send_l, send_r, send_t, recv_l, recv_r, recv_t, pass_send, pass_recv):
    row = lax.axis_index("row")
    loop = lax.axis_index("loop")
    core = loop % 2
    y_hi = loop // 2
    x = row // 8
    z = (row // 2) % 4
    y = y_hi * 2 + row % 2
    me = y_hi * 32 + row

    def target(o):
        tx = (x + o // 16) % 4
        ty = (y + (o // 4) % 4) % 4
        tz = (z + o % 4) % 4
        t_row = (tx * 4 + tz) * 2 + ty % 2
        return (ty // 2) * 32 + t_row, (t_row, (ty // 2) * 2 + core)

    barrier = pltpu.get_barrier_semaphore()

    def greet(o, carry):
        _, device = target(o)
        pl.semaphore_signal(barrier, inc=1, device_id=device, device_id_type=MESH)
        return carry

    lax.fori_loop(1, CHIPS, greet, 0)
    twin = (row, y_hi * 2 + (1 - core))
    pl.semaphore_signal(barrier, inc=1, device_id=twin, device_id_type=MESH)
    pl.semaphore_wait(barrier, CHIPS)

    def send_all(src, dst, send, recv):
        def body(n, carry):
            chip, device = target((n * 21) % CHIPS)
            pltpu.make_async_remote_copy(
                src.at[chip], dst.at[me], send, recv.at[y_hi], device_id=device, device_id_type=MESH
            ).start()
            return carry

        lax.fori_loop(1, CHIPS, body, 0)
        pltpu.make_async_copy(src.at[me], dst.at[me], recv.at[y_hi]).start()

    send_all(left_ref, own, send_l, recv_l)
    send_all(right_ref, right, send_r, recv_r)

    def half(ref, h):
        return ref.at[pl.ds(h * 32, 32)]

    passed = []
    for h in range(2):
        pltpu.make_async_copy(half(own, h), half(own, h), recv_l.at[h]).wait()
        copy = pltpu.make_async_remote_copy(
            half(own, h), half(other, h), pass_send.at[h], pass_recv.at[h],
            device_id=twin, device_id_type=MESH,
        )
        copy.start()
        passed.append(copy)

    def flip(ref, h, of):
        block = ref[pl.ds(h * 32, 32)].reshape(768, 384)
        flipped[h * 2 + of] = block.T

    for h in range(2):
        flip(own, h, core)
    for h in range(2):
        passed[h].wait()
        flip(other, h, 1 - core)

    for h in range(2):
        pltpu.make_async_copy(half(right, h), half(right, h), recv_r.at[h]).wait()

    lane = lax.broadcasted_iota(jnp.int32, (192, 128), 1)

    def multiply(n, carry):
        h = (y_hi + n // 4) % 2
        block = (x + 2 + n) % 4
        first = h * 32 + block * 8
        r = right[pl.ds(h * 32, 32)].reshape(768, 384)
        l = flipped[block]
        t0 = jnp.dot(l[0:192], r[:, 0:256], preferred_element_type=f32)
        t1 = jnp.dot(l[192:384], r[:, 128:384], preferred_element_type=f32)
        t1 = jnp.concatenate([t1[64:192], t1[0:64]], axis=0)
        mid = jnp.where(lane < 64, t0[:, 128:256], t1[:, 0:128])
        t = jnp.concatenate([t0[:, 0:128], mid, t1[:, 128:256]], axis=1)
        outgoing[pl.ds(first, 8)] = t.reshape(8, 3, 8, 384).astype(bf16)

        def ship(m, inner):
            chip = first + m

            @pl.when(chip != me)
            def _():
                t_row = block * 8 + m
                pltpu.make_async_remote_copy(
                    outgoing.at[chip], out_ref.at[me], send_t, recv_t,
                    device_id=(t_row, h * 2 + core), device_id_type=MESH,
                ).start()

            return inner

        lax.fori_loop(0, 8, ship, 0)
        return carry

    lax.fori_loop(0, 8, multiply, 0)
    pltpu.make_async_copy(outgoing.at[me], out_ref.at[me], recv_t).start()
    pltpu.make_async_copy(outgoing, out_ref, recv_t).wait()
    most = pl.ds(0, CHIPS - 1)
    pltpu.make_async_copy(left_ref.at[most], own.at[most], send_l).wait()
    pltpu.make_async_copy(right_ref.at[most], right.at[most], send_r).wait()
    pltpu.make_async_copy(outgoing.at[most], out_ref.at[most], send_t).wait()


def exchange(left, right):
    message = (CHIPS, 3, 8, 384)
    dma = pltpu.SemaphoreType.DMA
    return pl.pallas_call(
        exchange_kernel,
        name="exchange",
        out_shape=jax.ShapeDtypeStruct(message, bf16),
        in_specs=[pl.BlockSpec(memory_space=pl.ANY)] * 2,
        out_specs=pl.BlockSpec(memory_space=pl.ANY),
        scratch_shapes=[
            pltpu.VMEM(message, bf16),
            pltpu.VMEM(message, bf16),
            pltpu.VMEM(message, bf16),
            pltpu.VMEM((4, 384, 768), bf16),
            pltpu.VMEM(message, bf16),
            dma, dma, dma, dma((2,)), dma((2,)), dma, dma((2,)), dma((2,)),
        ],
        compiler_params=pltpu.CompilerParams(collective_id=0, has_side_effects=True),
    )(left, right)


def finish_kernel(t_ref, gate_ref, gain_ref, bias_ref, w_ref, out_ref, scale, shift, major):
    @pl.when(pl.program_id(0) == 0)
    def _():
        diagonal = (lax.broadcasted_iota(jnp.int32, (128, 128), 0)
                    == lax.broadcasted_iota(jnp.int32, (128, 128), 1))
        lane = lax.broadcasted_iota(jnp.int32, (64, 128), 1)
        for source, dest in ((gain_ref, scale), (bias_ref, shift)):
            column = jnp.sum(jnp.where(diagonal, source[...], 0.0), axis=1, keepdims=True)
            wide = jnp.broadcast_to(column, (128, 128))
            dest[:, 0:128] = wide[0:64]
            dest[:, 128:256] = jnp.where(lane < 64, wide[0:64], wide[64:128])
            dest[:, 256:384] = wide[64:128]

    def over_channels(values):
        total = jnp.sum(values, axis=0)
        ends = total[:, 0:128] + total[:, 256:384]
        mid = total[:, 128:256]
        mid = mid + pltpu.roll(mid, 64, 1)
        return jnp.concatenate([ends, mid, ends], axis=1) * (1.0 / 128)

    t = t_ref[:, 0].astype(f32)
    center = t - over_channels(t)[None]
    spread = over_channels(center * center)
    scaled = (center * lax.rsqrt(spread + epsilon)[None]).reshape(512, 384)
    for part in range(3):
        major[part] = scaled[:, 128 * part:128 * part + 128]
    lane = lax.broadcasted_iota(jnp.int32, (64, 128), 1)
    w = w_ref[...]
    for pair in range(4):
        mids = []
        for i in (2 * pair, 2 * pair + 1):
            mixed = [
                major[part, pl.ds(i, 64, stride=8), :] * scale[:, 128 * part:128 * part + 128]
                + shift[:, 128 * part:128 * part + 128]
                for part in range(3)
            ]
            mids.append(mixed[1])
            ends = jnp.concatenate([mixed[0], mixed[2]], axis=0).astype(bf16)
            wide = lax.dot_general(ends, w, TN, preferred_element_type=f32)
            out_ref[i, 0:128] = (gate_ref[i, 0:128] * wide).astype(bf16)
        top = jnp.where(lane < 64, mids[0], pltpu.roll(mids[1], 64, 1))
        low = jnp.where(lane < 64, pltpu.roll(mids[0], 64, 1), mids[1])
        both = jnp.concatenate([top, low], axis=0).astype(bf16)
        wide = lax.dot_general(both, w, TN, preferred_element_type=f32)
        for n in range(2):
            i = 2 * pair + n
            out_ref[i, 128:192] = (gate_ref[i, 128:192] * wide[64 * n:64 * n + 64]).astype(bf16)


def finish(triangle, gate, gain, bias, w_out):
    whole = lambda shape: pl.BlockSpec(shape, lambda i: (0,) * len(shape))
    return pl.pallas_call(
        finish_kernel,
        name="finish",
        grid=(3,),
        out_shape=jax.ShapeDtypeStruct((24, 192, 128), bf16),
        in_specs=[
            pl.BlockSpec((CHIPS, 1, 8, 384), lambda i: (0, i, 0, 0)),
            pl.BlockSpec((8, 192, 128), lambda i: (i, 0, 0)),
            whole((1, 128)), whole((1, 128)), whole((128, 128)),
        ],
        out_specs=pl.BlockSpec((8, 192, 128), lambda i: (i, 0, 0)),
        scratch_shapes=[
            pltpu.VMEM((64, 384), f32),
            pltpu.VMEM((64, 384), f32),
            pltpu.VMEM((3, 512, 128), f32),
        ],
        compiler_params=pltpu.CompilerParams(dimension_semantics=("arbitrary",)),
    )(triangle, gate, gain, bias, w_out)


def on_device(pair, ln_in_gain, ln_in_bias, w_proj, w_gate, ln_out_gain, ln_out_bias, w_out):
    left, right, gate = project(
        pair, ln_in_gain.reshape(1, 128), ln_in_bias.reshape(1, 128), w_proj, w_gate
    )
    triangle = exchange(left, right)
    return finish(
        triangle, gate, ln_out_gain.reshape(1, 128), ln_out_bias.reshape(1, 128), w_out
    )


def solution(mesh):
    return jax.shard_map(
        on_device,
        mesh=mesh,
        in_specs=(P("row", "loop", None), P(), P(), P(), P(), P(), P(), P()),
        out_specs=P("row", "loop", None),
        check_vma=False,
    )
```

```python
import jax
import jax.numpy as jnp
from jax import lax
from jax.experimental import pallas as pl
from jax.experimental.pallas import tpu as pltpu
from jax.sharding import PartitionSpec as P

epsilon = 1e-05
MESH = pl.DeviceIdType.MESH
f32 = jnp.float32
bf16 = jnp.bfloat16
CHIPS = 64
NT = (((1,), (1,)), ((), ()))
TN = (((0,), (0,)), ((), ()))


def normalize(values, gain, bias):
    center = values - jnp.mean(values, axis=-1, keepdims=True)
    spread = jnp.mean(center * center, axis=-1, keepdims=True)
    return center * lax.rsqrt(spread + epsilon) * gain + bias


def over_channels(values):
    total = jnp.sum(values, axis=0)
    ends = total[:, 0:128] + total[:, 256:384]
    mid = total[:, 128:256]
    mid = mid + pltpu.roll(mid, 64, 1)
    return jnp.concatenate([ends, mid, ends], axis=1) * (1.0 / 128)


def kernel(pair_ref, gain_ref, bias_ref, w_ref, wg_ref, out_gain_ref, out_bias_ref, wo_ref, out_ref,
           wide, tall, normed, gate, major, message, own, other, acc, mid0, out0, out1, got0, got1,
           scale, shift, mixing,
           send_m, recv_m, pass_send, pass_recv, send_t0, recv_t0, send_t1, recv_t1):
    row = lax.axis_index("row")
    loop = lax.axis_index("loop")
    core = loop % 2
    y_hi = loop // 2
    x = row // 8
    z = (row // 2) % 4
    y = y_hi * 2 + row % 2
    me = y_hi * 32 + row
    twin = (row, y_hi * 2 + (1 - core))

    def target(n):
        o = (n * 21) % CHIPS
        tx = (x + o // 16) % 4
        ty = (y + (o // 4) % 4) % 4
        tz = (z + o % 4) % 4
        t_row = (tx * 4 + tz) * 2 + ty % 2
        return (ty // 2) * 32 + t_row, (t_row, (ty // 2) * 2 + core)

    barrier = pltpu.get_barrier_semaphore()

    def greet(n, carry):
        _, device = target(n)
        pl.semaphore_signal(barrier, inc=1, device_id=device, device_id_type=MESH)
        return carry

    lax.fori_loop(1, CHIPS, greet, 0)
    pl.semaphore_signal(barrier, inc=1, device_id=twin, device_id_type=MESH)

    flipped = w_ref[...].astype(f32).T.astype(bf16)
    for g in range(2):
        for kind in range(4):
            part = flipped[128 * kind + 64 * g:128 * kind + 64 * g + 64]
            wide[g, pl.ds(64 * kind, 64)] = part
            tall[g, pl.ds(64 * (kind % 2), 64), pl.ds(128 * (kind // 2), 128)] = part

    def project(g, kc):
        for k in range(8):
            values = normed[8 * kc + k]
            head = values[0:128]
            rest = values[128:192]
            zero = jnp.zeros_like(rest)
            both = jnp.concatenate(
                [jnp.concatenate([rest, zero], axis=1), jnp.concatenate([zero, rest], axis=1)],
                axis=0,
            )
            a = lax.dot_general(wide[g], head, NT, preferred_element_type=f32)
            b = lax.dot_general(tall[g], both, NT, preferred_element_type=f32)
            rows = pl.ds(64 * k, 64)
            major[0, rows] = jax.nn.sigmoid(a[0:64]) * a[64:128]
            major[1, rows] = jax.nn.sigmoid(b[0:64]) * b[64:128]
            major[2, rows] = jax.nn.sigmoid(a[128:192]) * a[192:256]
        for c in range(CHIPS):
            for part in range(3):
                message[g, c, kc, :, pl.ds(128 * part, 128)] = (
                    major[part, pl.ds(c, 8, stride=64), :].astype(bf16)
                )

    def send_chunk(g, kc):
        def body(n, carry):
            chip, device = target(n)
            pltpu.make_async_remote_copy(
                message.at[g, chip, kc], own.at[g, me, kc], send_m.at[g], recv_m.at[g, kc],
                device_id=device, device_id_type=MESH,
            ).start()
            return carry

        lax.fori_loop(1, CHIPS, body, 0)
        pltpu.make_async_copy(message.at[g, me, kc], own.at[g, me, kc], recv_m.at[g, kc]).start()

    def first(kc):
        for k in range(8):
            values = pair_ref[8 * kc + k].astype(f32)
            normed[8 * kc + k] = normalize(values, gain_ref[...], bias_ref[...]).astype(bf16)
        project(0, kc)

    first(0)
    pl.semaphore_wait(barrier, CHIPS)
    send_chunk(0, 0)

    def rest_of_first(kc, carry):
        first(kc)
        send_chunk(0, kc)
        return carry

    lax.fori_loop(1, 3, rest_of_first, 0)

    def second(kc, carry):
        project(1, kc)
        send_chunk(1, kc)
        return carry

    lax.fori_loop(0, 3, second, 0)

    def open_gate(k, carry):
        gate[k] = jax.nn.sigmoid(jnp.dot(normed[k], wg_ref[...], preferred_element_type=f32))
        return carry

    lax.fori_loop(0, 24, open_gate, 0)

    diagonal = (lax.broadcasted_iota(jnp.int32, (128, 128), 0)
                == lax.broadcasted_iota(jnp.int32, (128, 128), 1))
    lane64 = lax.broadcasted_iota(jnp.int32, (64, 128), 1)
    lane192 = lax.broadcasted_iota(jnp.int32, (192, 128), 1)
    for source, dest in ((out_gain_ref, scale), (out_bias_ref, shift)):
        column = jnp.sum(jnp.where(diagonal, source[...], 0.0), axis=1, keepdims=True)
        spread_out = jnp.broadcast_to(column, (128, 128))
        dest[0] = spread_out[0:64]
        dest[1] = jnp.where(lane64 < 64, spread_out[0:64], spread_out[64:128])
        dest[2] = spread_out[64:128]

    def multiply(g, kc, left_ref, of):
        def block(h, carry):
            left = left_ref[g, pl.ds(h * 32, 32), kc, :, 0:256].reshape(256, 256).T[0:192]
            for j in range(2):
                right = own[g, 32 * j:32 * j + 32, kc, :, 128:384].reshape(256, 256)
                acc[h * 2 + of, j] += jnp.dot(left, right, preferred_element_type=f32)
            return carry

        lax.fori_loop(0, 2, block, 0)

    def gather(g):
        acc[...] = jnp.zeros_like(acc)

        def chunk(kc, carry):
            pltpu.make_async_copy(own.at[g, :, kc], own.at[g, :, kc], recv_m.at[g, kc]).wait()
            passing = pltpu.make_async_remote_copy(
                own.at[g, :, kc, :, pl.ds(0, 256)], other.at[g, :, kc],
                pass_send.at[g, kc], pass_recv.at[g, kc], device_id=twin, device_id_type=MESH,
            )
            passing.start()
            multiply(g, kc, own, core)
            passing.wait()
            multiply(g, kc, other, 1 - core)
            return carry

        lax.fori_loop(0, 3, chunk, 0)

    gather(0)

    def close_first(n, carry):
        block = n % 4
        j = n // 4
        t = acc[block, j]
        out0[pl.ds(j * 32 + block * 8, 8)] = t[:, 128:256].reshape(8, 3, 8, 128).astype(bf16)
        mid0[block, j] = pltpu.roll(t[:, 0:128], 64, 1)
        return carry

    lax.fori_loop(0, 8, close_first, 0)

    def ship_first(n, carry):
        chip, device = target(n)
        pltpu.make_async_remote_copy(
            out0.at[chip], got0.at[me], send_t0, recv_t0, device_id=device, device_id_type=MESH
        ).start()
        return carry

    lax.fori_loop(1, CHIPS, ship_first, 0)
    pltpu.make_async_copy(out0.at[me], got0.at[me], recv_t0).start()

    gather(1)

    def close_second(n, carry):
        block = n % 4
        j = n // 4
        t = acc[block, j]
        mid = jnp.where(lane192 < 64, mid0[block, j], t[:, 0:128])
        t = jnp.concatenate([mid, t[:, 128:256]], axis=1)
        out1[pl.ds(j * 32 + block * 8, 8)] = t.reshape(8, 3, 8, 256).astype(bf16)
        return carry

    lax.fori_loop(0, 8, close_second, 0)

    def ship_second(it, carry):
        def body(n, inner):
            chip, device = target(n)
            pltpu.make_async_remote_copy(
                out1.at[chip, it], got1.at[me, it], send_t1, recv_t1.at[it],
                device_id=device, device_id_type=MESH,
            ).start()
            return inner

        lax.fori_loop(1, CHIPS, body, 0)
        pltpu.make_async_copy(out1.at[me, it], got1.at[me, it], recv_t1.at[it]).start()
        return carry

    lax.fori_loop(0, 3, ship_second, 0)

    pltpu.make_async_copy(out0, got0, recv_t0).wait()

    def finish(it, carry):
        pltpu.make_async_copy(out1.at[:, it], got1.at[:, it], recv_t1.at[it]).wait()
        t = jnp.concatenate([got0[:, it], got1[:, it]], axis=-1).astype(f32)
        center = t - over_channels(t)[None]
        spread = over_channels(center * center)
        scaled = (center * lax.rsqrt(spread + epsilon)[None]).reshape(512, 384)
        for part in range(3):
            mixing[part] = scaled[:, 128 * part:128 * part + 128]
        w = wo_ref[...]
        for pair in range(4):
            mids = []
            for n in range(2):
                i = 2 * pair + n
                mixed = [
                    mixing[part, pl.ds(i, 64, stride=8), :] * scale[part] + shift[part]
                    for part in range(3)
                ]
                mids.append(mixed[1])
                ends = jnp.concatenate([mixed[0], mixed[2]], axis=0).astype(bf16)
                result = lax.dot_general(ends, w, TN, preferred_element_type=f32)
                k = 8 * it + i
                out_ref[k, 0:128] = (gate[k, 0:128] * result).astype(bf16)
            top = jnp.where(lane64 < 64, mids[0], pltpu.roll(mids[1], 64, 1))
            low = jnp.where(lane64 < 64, pltpu.roll(mids[0], 64, 1), mids[1])
            both = jnp.concatenate([top, low], axis=0).astype(bf16)
            result = lax.dot_general(both, w, TN, preferred_element_type=f32)
            for n in range(2):
                k = 8 * it + 2 * pair + n
                out_ref[k, 128:192] = (gate[k, 128:192] * result[64 * n:64 * n + 64]).astype(bf16)
        return carry

    lax.fori_loop(0, 3, finish, 0)

    most = pl.ds(0, CHIPS - 1)
    for g in range(2):
        pltpu.make_async_copy(message.at[g, most], own.at[g, most], send_m.at[g]).wait()
    pltpu.make_async_copy(out0.at[most], got0.at[most], send_t0).wait()
    pltpu.make_async_copy(out1.at[most], got1.at[most], send_t1).wait()


def on_device(pair, ln_in_gain, ln_in_bias, w_proj, w_gate, ln_out_gain, ln_out_bias, w_out):
    dma = pltpu.SemaphoreType.DMA
    vmem = pl.BlockSpec(memory_space=pltpu.VMEM)
    return pl.pallas_call(
        kernel,
        name="triangle",
        out_shape=jax.ShapeDtypeStruct((24, 192, 128), bf16),
        in_specs=[vmem] * 8,
        out_specs=vmem,
        scratch_shapes=[
            pltpu.VMEM((2, 256, 128), bf16),
            pltpu.VMEM((2, 128, 256), bf16),
            pltpu.VMEM((24, 192, 128), bf16),
            pltpu.VMEM((24, 192, 128), f32),
            pltpu.VMEM((3, 512, 128), f32),
            pltpu.VMEM((2, CHIPS, 3, 8, 384), bf16),
            pltpu.VMEM((2, CHIPS, 3, 8, 384), bf16),
            pltpu.VMEM((2, CHIPS, 3, 8, 256), bf16),
            pltpu.VMEM((4, 2, 192, 256), f32),
            pltpu.VMEM((4, 2, 192, 128), f32),
            pltpu.VMEM((CHIPS, 3, 8, 128), bf16),
            pltpu.VMEM((CHIPS, 3, 8, 256), bf16),
            pltpu.VMEM((CHIPS, 3, 8, 128), bf16),
            pltpu.VMEM((CHIPS, 3, 8, 256), bf16),
            pltpu.VMEM((3, 64, 128), f32),
            pltpu.VMEM((3, 64, 128), f32),
            pltpu.VMEM((3, 512, 128), f32),
            dma((2,)), dma((2, 3)), dma((2, 3)), dma((2, 3)), dma, dma, dma, dma((3,)),
        ],
        compiler_params=pltpu.CompilerParams(collective_id=0, has_side_effects=True),
    )(pair, ln_in_gain.reshape(1, 128), ln_in_bias.reshape(1, 128), w_proj, w_gate,
      ln_out_gain.reshape(1, 128), ln_out_bias.reshape(1, 128), w_out)


def solution(mesh):
    return jax.shard_map(
        on_device,
        mesh=mesh,
        in_specs=(P("row", "loop", None), P(), P(), P(), P(), P(), P(), P()),
        out_specs=P("row", "loop", None),
        check_vma=False,
    )
```

```python
import jax
import jax.numpy as jnp
from jax import lax
from jax.experimental import pallas as pl
from jax.experimental.pallas import tpu as pltpu
from jax.sharding import PartitionSpec as P

epsilon = 1e-05
MESH = pl.DeviceIdType.MESH
f32 = jnp.float32
bf16 = jnp.bfloat16
CHIPS = 64
NT = (((1,), (1,)), ((), ()))
TN = (((0,), (0,)), ((), ()))


def distance(o):
    return sum(min(d, 4 - d) for d in (o // 16, o // 4 % 4, o % 4))


FAR_FIRST = sorted(range(1, CHIPS), key=lambda o: (-distance(o), o * 21 % CHIPS))


def normalize(values, gain, bias):
    center = values - jnp.mean(values, axis=-1, keepdims=True)
    spread = jnp.mean(center * center, axis=-1, keepdims=True)
    return center * lax.rsqrt(spread + epsilon) * gain + bias


def over_channels(ends, mid):
    ends = jnp.sum(ends, axis=0)
    mid = jnp.sum(mid, axis=0)
    return ends * (1.0 / 128), (mid + pltpu.roll(mid, 64, 1)) * (1.0 / 128)


def kernel(pair_ref, gain_ref, bias_ref, w_ref, wg_ref, out_gain_ref, out_bias_ref, wo_ref, out_ref,
           wide, tall, normed, gate, major, sent_l, sent_r, own, other, right, turned, sent_t, got_t,
           scale, shift, mixing,
           send_l, recv_l, pass_send, pass_recv, send_r, recv_r, send_t, recv_t, recv_last):
    row = lax.axis_index("row")
    loop = lax.axis_index("loop")
    core = loop % 2
    y_hi = loop // 2
    x = row // 8
    z = (row // 2) % 4
    y = y_hi * 2 + row % 2
    me = y_hi * 32 + row
    twin = (row, y_hi * 2 + (1 - core))
    xs = [((x + d) % 4) * 8 for d in range(4)]
    zs = [((z + d) % 4) * 2 for d in range(4)]
    ys = [(y + d) % 4 for d in range(4)]
    y_his = [v // 2 for v in ys]
    y_los = [v % 2 for v in ys]

    def each_peer(act):
        for o in FAR_FIRST:
            dy = o // 4 % 4
            t_row = xs[o // 16] + zs[o % 4] + y_los[dy]
            act(y_his[dy] * 32 + t_row, (t_row, y_his[dy] * 2 + core))

    def send(src, dst, send_sem, recv_sem):
        def act(chip, device):
            pltpu.make_async_remote_copy(
                src(chip), dst, send_sem, recv_sem, device_id=device, device_id_type=MESH
            ).start()

        each_peer(act)
        pltpu.make_async_copy(src(me), dst, recv_sem).start()

    barrier = pltpu.get_barrier_semaphore()
    each_peer(lambda chip, device: pl.semaphore_signal(
        barrier, inc=1, device_id=device, device_id_type=MESH))
    pl.semaphore_signal(barrier, inc=1, device_id=twin, device_id_type=MESH)

    flipped = w_ref[...].astype(f32).T.astype(bf16)
    for side in range(2):
        wide[side] = flipped[256 * side:256 * side + 256]
        for kind in range(2):
            for half in range(2):
                at = 256 * side + 128 * kind + 64 * half
                tall[side, pl.ds(64 * kind, 64), pl.ds(128 * half, 128)] = flipped[at:at + 64]

    def project(side, kc):
        for k in range(8):
            values = normed[8 * kc + k]
            head = values[0:128]
            rest = values[128:192]
            zero = jnp.zeros_like(rest)
            both = jnp.concatenate(
                [jnp.concatenate([rest, zero], axis=1), jnp.concatenate([zero, rest], axis=1)],
                axis=0,
            )
            a = lax.dot_general(wide[side], head, NT, preferred_element_type=f32)
            b = lax.dot_general(tall[side], both, NT, preferred_element_type=f32)
            rows = pl.ds(64 * k, 64)
            ends = jax.nn.sigmoid(a[0:128]) * a[128:256]
            major[0, rows] = ends[0:64]
            major[1, rows] = jax.nn.sigmoid(b[0:64]) * b[64:128]
            major[2, rows] = ends[64:128]

    def column(part, c):
        return major[part, pl.ds(c, 8, stride=64), :].astype(bf16)

    def project_left(kc):
        for k in range(8):
            values = pair_ref[8 * kc + k].astype(f32)
            normed[8 * kc + k] = normalize(values, gain_ref[...], bias_ref[...]).astype(bf16)
        project(0, kc)
        for c in range(CHIPS):
            for part in range(3):
                sent_l[c, kc, :, pl.ds(128 * part, 128)] = column(part, c)

    def send_left(kc):
        send(lambda chip: sent_l.at[chip, kc], own.at[me, kc], send_l, recv_l.at[kc])

    project_left(0)
    pl.semaphore_wait(barrier, CHIPS)
    send_left(0)

    def rest_of_left(kc, carry):
        project_left(kc)
        send_left(kc)
        return carry

    lax.fori_loop(1, 3, rest_of_left, 0)

    def project_right(kc, carry):
        project(1, kc)
        for c in range(CHIPS):
            for part in range(3):
                sent_r[part, c, kc] = column(part, c)
        return carry

    lax.fori_loop(0, 3, project_right, 0)

    def send_right(part, carry):
        send(lambda chip: sent_r.at[part, chip], right.at[part, me], send_r.at[part],
             recv_r.at[part])
        return carry

    lax.fori_loop(0, 3, send_right, 0)

    def open_gate(k, carry):
        gate[k] = jax.nn.sigmoid(jnp.dot(normed[k], wg_ref[...], preferred_element_type=f32))
        return carry

    lax.fori_loop(0, 24, open_gate, 0)

    diagonal = (lax.broadcasted_iota(jnp.int32, (128, 128), 0)
                == lax.broadcasted_iota(jnp.int32, (128, 128), 1))
    lane64 = lax.broadcasted_iota(jnp.int32, (64, 128), 1)
    for source, dest in ((out_gain_ref, scale), (out_bias_ref, shift)):
        one = jnp.sum(jnp.where(diagonal, source[...], 0.0), axis=1, keepdims=True)
        spread_out = jnp.broadcast_to(one, (128, 128))
        dest[0] = spread_out[0:64]
        dest[1] = jnp.where(lane64 < 64, spread_out[0:64], spread_out[64:128])
        dest[2] = spread_out[64:128]

    def turn(ref, kc, of):
        def block(h, carry):
            t = ref[pl.ds(h * 32, 32), kc].reshape(256, 384).T
            first = (h * 2 + of) * 192
            lanes = pl.ds(pl.multiple_of(kc * 256, 256), 256)
            turned[0, pl.ds(pl.multiple_of(first, 64), 192), lanes] = t[0:192]
            turned[1, pl.ds(pl.multiple_of(first + 128, 64), 64), lanes] = t[192:256]
            turned[1, pl.ds(pl.multiple_of(first, 64), 128), lanes] = t[256:384]
            return carry

        lax.fori_loop(0, 2, block, 0)

    def take_left(kc, carry):
        pltpu.make_async_copy(own.at[:, kc], own.at[:, kc], recv_l.at[kc]).wait()
        passing = pltpu.make_async_remote_copy(
            own.at[:, kc], other.at[:, kc], pass_send.at[kc], pass_recv.at[kc],
            device_id=twin, device_id_type=MESH,
        )
        passing.start()
        turn(own, kc, core)
        passing.wait()
        turn(other, kc, 1 - core)
        return carry

    lax.fori_loop(0, 3, take_left, 0)

    def factor(part):
        pltpu.make_async_copy(sent_r.at[part], right.at[part], recv_r.at[part]).wait()
        return [
            jnp.concatenate(
                [right[part, 32 * j:32 * j + 32, kc].reshape(256, 128) for j in range(2)], axis=1
            )
            for kc in range(3)
        ]

    def multiply(channel, factors):
        return sum(
            jnp.dot(turned[channel, :, 256 * kc:256 * kc + 256], factors[kc],
                    preferred_element_type=f32)
            for kc in range(3)
        )

    def keep(part, j, t):
        sent_t[part, 32 * j:32 * j + 32] = t.reshape(32, 3, 8, 128).astype(bf16)

    def send_part(part):
        send(lambda chip: sent_t.at[part, chip], got_t.at[part, me], send_t.at[part],
             recv_t.at[part])

    factors = factor(0)
    t = multiply(0, factors)
    for j in range(2):
        keep(0, j, t[:, 128 * j:128 * j + 128])
    send_part(0)

    factors = factor(1)
    t0 = multiply(0, factors)
    t1 = multiply(1, factors)
    lane768 = lax.broadcasted_iota(jnp.int32, (768, 128), 1)
    for j in range(2):
        lanes = slice(128 * j, 128 * j + 128)
        keep(1, j, jnp.where(lane768 < 64, t0[:, lanes], t1[:, lanes]))
    send_part(1)

    factors = factor(2)
    t = multiply(1, factors)
    for j in range(2):
        keep(2, j, t[:, 128 * j:128 * j + 128])

    def send_last(it, carry):
        send(lambda chip: sent_t.at[2, chip, it], got_t.at[2, me, it], send_t.at[2],
             recv_last.at[it])
        return carry

    lax.fori_loop(0, 3, send_last, 0)

    for part in range(2):
        pltpu.make_async_copy(sent_t.at[part], got_t.at[part], recv_t.at[part]).wait()

    def finish(it, carry):
        pltpu.make_async_copy(sent_t.at[2, :, it], got_t.at[2, :, it], recv_last.at[it]).wait()
        t0, mid, t2 = [got_t[part, :, it].astype(f32) for part in range(3)]
        ends_mean, mid_mean = over_channels(t0 + t2, mid)
        t0 = t0 - ends_mean[None]
        t2 = t2 - ends_mean[None]
        mid = mid - mid_mean[None]
        ends_spread, mid_spread = over_channels(t0 * t0 + t2 * t2, mid * mid)
        ends_root = lax.rsqrt(ends_spread + epsilon)[None]
        mid_root = lax.rsqrt(mid_spread + epsilon)[None]
        mixing[0] = (t0 * ends_root).reshape(512, 128)
        mixing[1] = (mid * mid_root).reshape(512, 128)
        mixing[2] = (t2 * ends_root).reshape(512, 128)
        w = wo_ref[...]
        for pair in range(4):
            mids = []
            for n in range(2):
                i = 2 * pair + n
                mixed = [
                    mixing[part, pl.ds(i, 64, stride=8), :] * scale[part] + shift[part]
                    for part in range(3)
                ]
                mids.append(mixed[1])
                ends = jnp.concatenate([mixed[0], mixed[2]], axis=0).astype(bf16)
                result = lax.dot_general(ends, w, TN, preferred_element_type=f32)
                k = 8 * it + i
                out_ref[k, 0:128] = (gate[k, 0:128] * result).astype(bf16)
            top = jnp.where(lane64 < 64, mids[0], pltpu.roll(mids[1], 64, 1))
            low = jnp.where(lane64 < 64, pltpu.roll(mids[0], 64, 1), mids[1])
            both = jnp.concatenate([top, low], axis=0).astype(bf16)
            result = lax.dot_general(both, w, TN, preferred_element_type=f32)
            for n in range(2):
                k = 8 * it + 2 * pair + n
                out_ref[k, 128:192] = (gate[k, 128:192] * result[64 * n:64 * n + 64]).astype(bf16)
        return carry

    lax.fori_loop(0, 3, finish, 0)

    most = pl.ds(0, CHIPS - 1)
    pltpu.make_async_copy(sent_l.at[most], own.at[most], send_l).wait()
    for part in range(3):
        pltpu.make_async_copy(sent_r.at[part, most], right.at[part, most], send_r.at[part]).wait()
        pltpu.make_async_copy(sent_t.at[part, most], got_t.at[part, most], send_t.at[part]).wait()


def on_device(pair, ln_in_gain, ln_in_bias, w_proj, w_gate, ln_out_gain, ln_out_bias, w_out):
    dma = pltpu.SemaphoreType.DMA
    vmem = pl.BlockSpec(memory_space=pltpu.VMEM)
    return pl.pallas_call(
        kernel,
        name="triangle",
        out_shape=jax.ShapeDtypeStruct((24, 192, 128), bf16),
        in_specs=[vmem] * 8,
        out_specs=vmem,
        scratch_shapes=[
            pltpu.VMEM((2, 256, 128), bf16),
            pltpu.VMEM((2, 128, 256), bf16),
            pltpu.VMEM((24, 192, 128), bf16),
            pltpu.VMEM((24, 192, 128), f32),
            pltpu.VMEM((3, 512, 128), f32),
            pltpu.VMEM((CHIPS, 3, 8, 384), bf16),
            pltpu.VMEM((3, CHIPS, 3, 8, 128), bf16),
            pltpu.VMEM((CHIPS, 3, 8, 384), bf16),
            pltpu.VMEM((CHIPS, 3, 8, 384), bf16),
            pltpu.VMEM((3, CHIPS, 3, 8, 128), bf16),
            pltpu.VMEM((2, 768, 768), bf16),
            pltpu.VMEM((3, CHIPS, 3, 8, 128), bf16),
            pltpu.VMEM((3, CHIPS, 3, 8, 128), bf16),
            pltpu.VMEM((3, 64, 128), f32),
            pltpu.VMEM((3, 64, 128), f32),
            pltpu.VMEM((3, 512, 128), f32),
            dma, dma((3,)), dma((3,)), dma((3,)), dma((3,)), dma((3,)), dma((3,)), dma((3,)), dma((3,)),
        ],
        compiler_params=pltpu.CompilerParams(collective_id=0, has_side_effects=True),
    )(pair, ln_in_gain.reshape(1, 128), ln_in_bias.reshape(1, 128), w_proj, w_gate,
      ln_out_gain.reshape(1, 128), ln_out_bias.reshape(1, 128), w_out)


def solution(mesh):
    return jax.shard_map(
        on_device,
        mesh=mesh,
        in_specs=(P("row", "loop", None), P(), P(), P(), P(), P(), P(), P()),
        out_specs=P("row", "loop", None),
        check_vma=False,
    )
```

```python
import jax
import jax.numpy as jnp
from jax import lax
from jax.experimental import pallas as pl
from jax.experimental.pallas import tpu as pltpu
from jax.sharding import PartitionSpec as P

epsilon = 1e-05
MESH = pl.DeviceIdType.MESH
f32 = jnp.float32
bf16 = jnp.bfloat16
CHIPS = 64
NT = (((1,), (1,)), ((), ()))
TN = (((0,), (0,)), ((), ()))


def distance(o):
    return sum(min(d, 4 - d) for d in (o // 16, o // 4 % 4, o % 4))


FAR_FIRST = sorted(range(1, CHIPS), key=lambda o: (-distance(o), o * 21 % CHIPS))


def normalize(values, gain, bias):
    center = values - jnp.mean(values, axis=-1, keepdims=True)
    spread = jnp.mean(center * center, axis=-1, keepdims=True)
    return center * lax.rsqrt(spread + epsilon) * gain + bias


def over_channels(ends, mid):
    ends = jnp.sum(ends, axis=0)
    mid = jnp.sum(mid, axis=0)
    return ends * (1.0 / 128), (mid + pltpu.roll(mid, 64, 1)) * (1.0 / 128)


def kernel(pair_hbm, gain_hbm, bias_hbm, w_hbm, wg_hbm, out_gain_hbm, out_bias_hbm, wo_hbm, out_ref,
           pair_ref, gain_ref, bias_ref, w_ref, wg_ref, out_gain_ref, out_bias_ref, wo_ref,
           wide, tall, normed, gate, major, sent_l, sent_r, own, other, right, turned, sent_t, got_t,
           scale, shift, mixing,
           load, load_pair, send_l, recv_l, pass_send, pass_recv, send_r, recv_r, send_t, recv_t, recv_last):
    def rows_of(kc):
        rows = pl.ds(pl.multiple_of(kc * 8, 8), 8)
        return pltpu.make_async_copy(pair_hbm.at[rows], pair_ref.at[rows], load_pair.at[kc])

    loads = [
        pltpu.make_async_copy(src, dst, load.at[n])
        for n, (src, dst) in enumerate((
            (w_hbm, w_ref), (gain_hbm, gain_ref), (bias_hbm, bias_ref), (wg_hbm, wg_ref),
            (out_gain_hbm, out_gain_ref), (out_bias_hbm, out_bias_ref), (wo_hbm, wo_ref),
        ))
    ]
    loads[0].start()
    for kc in range(3):
        rows_of(kc).start()
    for copy in loads[1:]:
        copy.start()

    row = lax.axis_index("row")
    loop = lax.axis_index("loop")
    core = loop % 2
    y_hi = loop // 2
    x = row // 8
    z = (row // 2) % 4
    y = y_hi * 2 + row % 2
    me = y_hi * 32 + row
    twin = (row, y_hi * 2 + (1 - core))
    xs = [((x + d) % 4) * 8 for d in range(4)]
    zs = [((z + d) % 4) * 2 for d in range(4)]
    ys = [(y + d) % 4 for d in range(4)]
    y_his = [v // 2 for v in ys]
    y_los = [v % 2 for v in ys]

    def each_peer(act):
        for o in FAR_FIRST:
            dy = o // 4 % 4
            t_row = xs[o // 16] + zs[o % 4] + y_los[dy]
            act(y_his[dy] * 32 + t_row, (t_row, y_his[dy] * 2 + core))

    def send(src, dst, send_sem, recv_sem):
        def act(chip, device):
            pltpu.make_async_remote_copy(
                src(chip), dst, send_sem, recv_sem, device_id=device, device_id_type=MESH
            ).start()

        each_peer(act)
        pltpu.make_async_copy(src(me), dst, recv_sem).start()

    barrier = pltpu.get_barrier_semaphore()
    each_peer(lambda chip, device: pl.semaphore_signal(
        barrier, inc=1, device_id=device, device_id_type=MESH))
    pl.semaphore_signal(barrier, inc=1, device_id=twin, device_id_type=MESH)

    def flip(side):
        flipped = w_ref[:, 256 * side:256 * side + 256].astype(f32).T.astype(bf16)
        wide[side] = flipped
        for kind in range(2):
            for half in range(2):
                at = 128 * kind + 64 * half
                tall[side, pl.ds(64 * kind, 64), pl.ds(128 * half, 128)] = flipped[at:at + 64]

    for copy in loads[0:3]:
        copy.wait()
    flip(0)

    def project(side, kc):
        for k in range(8):
            values = normed[8 * kc + k]
            head = values[0:128]
            rest = values[128:192]
            zero = jnp.zeros_like(rest)
            both = jnp.concatenate(
                [jnp.concatenate([rest, zero], axis=1), jnp.concatenate([zero, rest], axis=1)],
                axis=0,
            )
            a = lax.dot_general(wide[side], head, NT, preferred_element_type=f32)
            b = lax.dot_general(tall[side], both, NT, preferred_element_type=f32)
            rows = pl.ds(64 * k, 64)
            ends = jax.nn.sigmoid(a[0:128]) * a[128:256]
            major[0, rows] = ends[0:64]
            major[1, rows] = jax.nn.sigmoid(b[0:64]) * b[64:128]
            major[2, rows] = ends[64:128]

    def column(part, c):
        return major[part, pl.ds(c, 8, stride=64), :].astype(bf16)

    def project_left(kc):
        rows_of(kc).wait()
        for k in range(8):
            values = pair_ref[8 * kc + k].astype(f32)
            normed[8 * kc + k] = normalize(values, gain_ref[...], bias_ref[...]).astype(bf16)
        project(0, kc)
        for c in range(CHIPS):
            for part in range(3):
                sent_l[c, kc, :, pl.ds(128 * part, 128)] = column(part, c)

    def send_left(kc):
        send(lambda chip: sent_l.at[chip, kc], own.at[me, kc], send_l, recv_l.at[kc])

    project_left(0)
    pl.semaphore_wait(barrier, CHIPS)
    send_left(0)

    def rest_of_left(kc, carry):
        project_left(kc)
        send_left(kc)
        return carry

    lax.fori_loop(1, 3, rest_of_left, 0)

    flip(1)

    def project_right(kc, carry):
        project(1, kc)
        for c in range(CHIPS):
            for part in range(3):
                sent_r[part, c, kc] = column(part, c)
        return carry

    lax.fori_loop(0, 3, project_right, 0)

    def send_right(part, carry):
        send(lambda chip: sent_r.at[part, chip], right.at[part, me], send_r.at[part],
             recv_r.at[part])
        return carry

    lax.fori_loop(0, 3, send_right, 0)

    for copy in loads[3:]:
        copy.wait()

    def open_gate(k, carry):
        gate[k] = jax.nn.sigmoid(jnp.dot(normed[k], wg_ref[...], preferred_element_type=f32))
        return carry

    lax.fori_loop(0, 24, open_gate, 0)

    diagonal = (lax.broadcasted_iota(jnp.int32, (128, 128), 0)
                == lax.broadcasted_iota(jnp.int32, (128, 128), 1))
    lane64 = lax.broadcasted_iota(jnp.int32, (64, 128), 1)
    for source, dest in ((out_gain_ref, scale), (out_bias_ref, shift)):
        one = jnp.sum(jnp.where(diagonal, source[...], 0.0), axis=1, keepdims=True)
        spread_out = jnp.broadcast_to(one, (128, 128))
        dest[0] = spread_out[0:64]
        dest[1] = jnp.where(lane64 < 64, spread_out[0:64], spread_out[64:128])
        dest[2] = spread_out[64:128]

    def turn(ref, kc, of):
        def block(h, carry):
            t = ref[pl.ds(h * 32, 32), kc].reshape(256, 384).T
            first = (h * 2 + of) * 192
            lanes = pl.ds(pl.multiple_of(kc * 256, 256), 256)
            turned[0, pl.ds(pl.multiple_of(first, 64), 192), lanes] = t[0:192]
            turned[1, pl.ds(pl.multiple_of(first + 128, 64), 64), lanes] = t[192:256]
            turned[1, pl.ds(pl.multiple_of(first, 64), 128), lanes] = t[256:384]
            return carry

        lax.fori_loop(0, 2, block, 0)

    def take_left(kc, carry):
        pltpu.make_async_copy(own.at[:, kc], own.at[:, kc], recv_l.at[kc]).wait()
        passing = pltpu.make_async_remote_copy(
            own.at[:, kc], other.at[:, kc], pass_send.at[kc], pass_recv.at[kc],
            device_id=twin, device_id_type=MESH,
        )
        passing.start()
        turn(own, kc, core)
        passing.wait()
        turn(other, kc, 1 - core)
        return carry

    lax.fori_loop(0, 3, take_left, 0)

    def factor(part):
        pltpu.make_async_copy(sent_r.at[part], right.at[part], recv_r.at[part]).wait()
        return [
            jnp.concatenate(
                [right[part, 32 * j:32 * j + 32, kc].reshape(256, 128) for j in range(2)], axis=1
            )
            for kc in range(3)
        ]

    def multiply(channel, factors):
        return sum(
            jnp.dot(turned[channel, :, 256 * kc:256 * kc + 256], factors[kc],
                    preferred_element_type=f32)
            for kc in range(3)
        )

    def keep(part, j, t):
        sent_t[part, 32 * j:32 * j + 32] = t.reshape(32, 3, 8, 128).astype(bf16)

    def send_part(part):
        send(lambda chip: sent_t.at[part, chip], got_t.at[part, me], send_t.at[part],
             recv_t.at[part])

    factors = factor(0)
    t = multiply(0, factors)
    for j in range(2):
        keep(0, j, t[:, 128 * j:128 * j + 128])
    send_part(0)

    factors = factor(1)
    t0 = multiply(0, factors)
    t1 = multiply(1, factors)
    lane768 = lax.broadcasted_iota(jnp.int32, (768, 128), 1)
    for j in range(2):
        lanes = slice(128 * j, 128 * j + 128)
        keep(1, j, jnp.where(lane768 < 64, t0[:, lanes], t1[:, lanes]))
    send_part(1)

    factors = factor(2)
    t = multiply(1, factors)
    for j in range(2):
        keep(2, j, t[:, 128 * j:128 * j + 128])

    def send_last(it, carry):
        send(lambda chip: sent_t.at[2, chip, it], got_t.at[2, me, it], send_t.at[2],
             recv_last.at[it])
        return carry

    lax.fori_loop(0, 3, send_last, 0)

    for part in range(2):
        pltpu.make_async_copy(sent_t.at[part], got_t.at[part], recv_t.at[part]).wait()

    def finish(it, carry):
        pltpu.make_async_copy(sent_t.at[2, :, it], got_t.at[2, :, it], recv_last.at[it]).wait()
        t0, mid, t2 = [got_t[part, :, it].astype(f32) for part in range(3)]
        ends_mean, mid_mean = over_channels(t0 + t2, mid)
        t0 = t0 - ends_mean[None]
        t2 = t2 - ends_mean[None]
        mid = mid - mid_mean[None]
        ends_spread, mid_spread = over_channels(t0 * t0 + t2 * t2, mid * mid)
        ends_root = lax.rsqrt(ends_spread + epsilon)[None]
        mid_root = lax.rsqrt(mid_spread + epsilon)[None]
        mixing[0] = (t0 * ends_root).reshape(512, 128)
        mixing[1] = (mid * mid_root).reshape(512, 128)
        mixing[2] = (t2 * ends_root).reshape(512, 128)
        w = wo_ref[...]
        for pair in range(4):
            mids = []
            for n in range(2):
                i = 2 * pair + n
                mixed = [
                    mixing[part, pl.ds(i, 64, stride=8), :] * scale[part] + shift[part]
                    for part in range(3)
                ]
                mids.append(mixed[1])
                ends = jnp.concatenate([mixed[0], mixed[2]], axis=0).astype(bf16)
                result = lax.dot_general(ends, w, TN, preferred_element_type=f32)
                k = 8 * it + i
                out_ref[k, 0:128] = (gate[k, 0:128] * result).astype(bf16)
            top = jnp.where(lane64 < 64, mids[0], pltpu.roll(mids[1], 64, 1))
            low = jnp.where(lane64 < 64, pltpu.roll(mids[0], 64, 1), mids[1])
            both = jnp.concatenate([top, low], axis=0).astype(bf16)
            result = lax.dot_general(both, w, TN, preferred_element_type=f32)
            for n in range(2):
                k = 8 * it + 2 * pair + n
                out_ref[k, 128:192] = (gate[k, 128:192] * result[64 * n:64 * n + 64]).astype(bf16)
        return carry

    lax.fori_loop(0, 3, finish, 0)

    most = pl.ds(0, CHIPS - 1)
    pltpu.make_async_copy(sent_l.at[most], own.at[most], send_l).wait()
    for part in range(3):
        pltpu.make_async_copy(sent_r.at[part, most], right.at[part, most], send_r.at[part]).wait()
        pltpu.make_async_copy(sent_t.at[part, most], got_t.at[part, most], send_t.at[part]).wait()


def on_device(pair, ln_in_gain, ln_in_bias, w_proj, w_gate, ln_out_gain, ln_out_bias, w_out):
    dma = pltpu.SemaphoreType.DMA
    vmem = pl.BlockSpec(memory_space=pltpu.VMEM)
    return pl.pallas_call(
        kernel,
        name="triangle",
        out_shape=pltpu.VMEM((24, 192, 128), bf16),
        in_specs=[pl.BlockSpec(memory_space=pl.ANY)] * 8,
        out_specs=vmem,
        scratch_shapes=[
            pltpu.VMEM((24, 192, 128), bf16),
            pltpu.VMEM((1, 128), f32),
            pltpu.VMEM((1, 128), f32),
            pltpu.VMEM((128, 512), bf16),
            pltpu.VMEM((128, 128), bf16),
            pltpu.VMEM((1, 128), f32),
            pltpu.VMEM((1, 128), f32),
            pltpu.VMEM((128, 128), bf16),
            pltpu.VMEM((2, 256, 128), bf16),
            pltpu.VMEM((2, 128, 256), bf16),
            pltpu.VMEM((24, 192, 128), bf16),
            pltpu.VMEM((24, 192, 128), f32),
            pltpu.VMEM((3, 512, 128), f32),
            pltpu.VMEM((CHIPS, 3, 8, 384), bf16),
            pltpu.VMEM((3, CHIPS, 3, 8, 128), bf16),
            pltpu.VMEM((CHIPS, 3, 8, 384), bf16),
            pltpu.VMEM((CHIPS, 3, 8, 384), bf16),
            pltpu.VMEM((3, CHIPS, 3, 8, 128), bf16),
            pltpu.VMEM((2, 768, 768), bf16),
            pltpu.VMEM((3, CHIPS, 3, 8, 128), bf16),
            pltpu.VMEM((3, CHIPS, 3, 8, 128), bf16),
            pltpu.VMEM((3, 64, 128), f32),
            pltpu.VMEM((3, 64, 128), f32),
            pltpu.VMEM((3, 512, 128), f32),
            dma((7,)), dma((3,)), dma, dma((3,)), dma((3,)), dma((3,)), dma((3,)), dma((3,)), dma((3,)), dma((3,)), dma((3,)),
        ],
        compiler_params=pltpu.CompilerParams(collective_id=0, has_side_effects=True),
    )(pair, ln_in_gain.reshape(1, 128), ln_in_bias.reshape(1, 128), w_proj, w_gate,
      ln_out_gain.reshape(1, 128), ln_out_bias.reshape(1, 128), w_out)


def solution(mesh):
    return jax.shard_map(
        on_device,
        mesh=mesh,
        in_specs=(P("row", "loop", None), P(), P(), P(), P(), P(), P(), P()),
        out_specs=P("row", "loop", None),
        check_vma=False,
    )
```

```python
import jax
import jax.numpy as jnp
from jax import lax
from jax.experimental import pallas as pl
from jax.experimental.pallas import tpu as pltpu
from jax.sharding import PartitionSpec as P

epsilon = 1e-05
MESH = pl.DeviceIdType.MESH
f32 = jnp.float32
bf16 = jnp.bfloat16
CHIPS = 64
NT = (((1,), (1,)), ((), ()))
TN = (((0,), (0,)), ((), ()))


def distance(o):
    return sum(min(d, 4 - d) for d in (o // 16, o // 4 % 4, o % 4))


FAR_FIRST = sorted(range(1, CHIPS), key=lambda o: (-distance(o), o * 21 % CHIPS))
MIXED = [o * 21 % CHIPS for o in range(1, CHIPS)]


def normalize(values, gain, bias):
    center = values - jnp.mean(values, axis=-1, keepdims=True)
    spread = jnp.mean(center * center, axis=-1, keepdims=True)
    return center * lax.rsqrt(spread + epsilon) * gain + bias


def kernel(pair_hbm, gain_hbm, bias_hbm, w_hbm, wg_hbm, out_gain_hbm, out_bias_hbm, wo_hbm, out_ref,
           pair_ref, gain_ref, bias_ref, w_ref, wg_ref, out_gain_ref, out_bias_ref, wo_ref,
           wide, tall, normed, gate, major, sent_l, sent_r, own, other, right, turned, sent_t, got_t,
           scale, shift, mixing,
           load, load_pair, send_l, recv_l, pass_send, pass_recv, send_r, recv_r, send_t, recv_t, recv_last):
    def rows_of(kc):
        rows = pl.ds(pl.multiple_of(kc * 8, 8), 8)
        return pltpu.make_async_copy(pair_hbm.at[rows], pair_ref.at[rows], load_pair.at[kc])

    loads = [
        pltpu.make_async_copy(src, dst, load.at[n])
        for n, (src, dst) in enumerate((
            (w_hbm, w_ref), (gain_hbm, gain_ref), (bias_hbm, bias_ref), (wg_hbm, wg_ref),
            (out_gain_hbm, out_gain_ref), (out_bias_hbm, out_bias_ref), (wo_hbm, wo_ref),
        ))
    ]
    loads[0].start()
    for kc in range(3):
        rows_of(kc).start()
    for copy in loads[1:]:
        copy.start()

    row = lax.axis_index("row")
    loop = lax.axis_index("loop")
    core = loop % 2
    y_hi = loop // 2
    x = row // 8
    z = (row // 2) % 4
    y = y_hi * 2 + row % 2
    me = y_hi * 32 + row
    twin = (row, y_hi * 2 + (1 - core))
    xs = [((x + d) % 4) * 8 for d in range(4)]
    zs = [((z + d) % 4) * 2 for d in range(4)]
    ys = [(y + d) % 4 for d in range(4)]
    y_his = [v // 2 for v in ys]
    y_los = [v % 2 for v in ys]

    def each_peer(act, order):
        for o in order:
            dy = o // 4 % 4
            t_row = xs[o // 16] + zs[o % 4] + y_los[dy]
            act(y_his[dy] * 32 + t_row, (t_row, y_his[dy] * 2 + core))

    def send(src, dst, send_sem, recv_sem, order=MIXED):
        def act(chip, device):
            pltpu.make_async_remote_copy(
                src(chip), dst, send_sem, recv_sem, device_id=device, device_id_type=MESH
            ).start()

        each_peer(act, order)
        pltpu.make_async_copy(src(me), dst, recv_sem).start()

    barrier = pltpu.get_barrier_semaphore()
    each_peer(lambda chip, device: pl.semaphore_signal(
        barrier, inc=1, device_id=device, device_id_type=MESH), FAR_FIRST)
    pl.semaphore_signal(barrier, inc=1, device_id=twin, device_id_type=MESH)

    def flip(side):
        flipped = w_ref[:, 256 * side:256 * side + 256].astype(f32).T.astype(bf16)
        wide[side] = flipped
        for kind in range(2):
            for half in range(2):
                at = 128 * kind + 64 * half
                tall[side, pl.ds(64 * kind, 64), pl.ds(128 * half, 128)] = flipped[at:at + 64]

    for copy in loads[0:3]:
        copy.wait()
    flip(0)

    def project(side, kc):
        for k in range(8):
            values = normed[8 * kc + k]
            head = values[0:128]
            rest = values[128:192]
            zero = jnp.zeros_like(rest)
            both = jnp.concatenate(
                [jnp.concatenate([rest, zero], axis=1), jnp.concatenate([zero, rest], axis=1)],
                axis=0,
            )
            a = lax.dot_general(wide[side], head, NT, preferred_element_type=f32)
            b = lax.dot_general(tall[side], both, NT, preferred_element_type=f32)
            rows = pl.ds(64 * k, 64)
            ends = jax.nn.sigmoid(a[0:128]) * a[128:256]
            major[0, rows] = ends[0:64]
            major[1, rows] = jax.nn.sigmoid(b[0:64]) * b[64:128]
            major[2, rows] = ends[64:128]

    def column(part, c):
        return major[part, pl.ds(c, 8, stride=64), :].astype(bf16)

    def project_left(kc):
        rows_of(kc).wait()
        for k in range(8):
            values = pair_ref[8 * kc + k].astype(f32)
            normed[8 * kc + k] = normalize(values, gain_ref[...], bias_ref[...]).astype(bf16)
        project(0, kc)
        for c in range(CHIPS):
            for part in range(3):
                sent_l[c, kc, :, pl.ds(128 * part, 128)] = column(part, c)

    def send_left(kc):
        send(lambda chip: sent_l.at[chip, kc], own.at[me, kc], send_l, recv_l.at[kc])

    project_left(0)
    pl.semaphore_wait(barrier, CHIPS)
    send_left(0)

    def rest_of_left(kc, carry):
        project_left(kc)
        send_left(kc)
        return carry

    lax.fori_loop(1, 3, rest_of_left, 0)

    flip(1)

    def project_right(kc, carry):
        project(1, kc)
        for c in range(CHIPS):
            for part in range(3):
                sent_r[part, c, kc] = column(part, c)
        return carry

    lax.fori_loop(0, 3, project_right, 0)

    def send_right(part, carry):
        send(lambda chip: sent_r.at[part, chip], right.at[part, me], send_r.at[part],
             recv_r.at[part])
        return carry

    for copy in loads[3:]:
        copy.wait()

    def open_gate(k, carry):
        gate[k] = jax.nn.sigmoid(jnp.dot(normed[k], wg_ref[...], preferred_element_type=f32))
        return carry

    def open_gates():
        lax.fori_loop(0, 24, open_gate, 0)

    pl.when(core == 1)(open_gates)
    lax.fori_loop(0, 3, send_right, 0)
    pl.when(core == 0)(open_gates)


    diagonal = (lax.broadcasted_iota(jnp.int32, (128, 128), 0)
                == lax.broadcasted_iota(jnp.int32, (128, 128), 1))
    lane64 = lax.broadcasted_iota(jnp.int32, (64, 128), 1)
    for source, dest in ((out_gain_ref, scale), (out_bias_ref, shift)):
        one = jnp.sum(jnp.where(diagonal, source[...], 0.0), axis=1, keepdims=True)
        spread_out = jnp.broadcast_to(one, (128, 128))
        dest[0] = spread_out[0:64]
        dest[1] = jnp.where(lane64 < 64, spread_out[0:64], spread_out[64:128])
        dest[2] = spread_out[64:128]

    def turn(ref, kc, of):
        def block(h, carry):
            t = ref[pl.ds(h * 32, 32), kc].reshape(256, 384).T
            first = (h * 2 + of) * 192
            lanes = pl.ds(pl.multiple_of(kc * 256, 256), 256)
            turned[0, pl.ds(pl.multiple_of(first, 64), 192), lanes] = t[0:192]
            turned[1, pl.ds(pl.multiple_of(first + 128, 64), 64), lanes] = t[192:256]
            turned[1, pl.ds(pl.multiple_of(first, 64), 128), lanes] = t[256:384]
            return carry

        lax.fori_loop(0, 2, block, 0)

    def take_left(kc, carry):
        pltpu.make_async_copy(own.at[:, kc], own.at[:, kc], recv_l.at[kc]).wait()
        passing = pltpu.make_async_remote_copy(
            own.at[:, kc], other.at[:, kc], pass_send.at[kc], pass_recv.at[kc],
            device_id=twin, device_id_type=MESH,
        )
        passing.start()
        turn(own, kc, core)
        passing.wait()
        turn(other, kc, 1 - core)
        return carry

    lax.fori_loop(0, 3, take_left, 0)

    def factor(part):
        pltpu.make_async_copy(sent_r.at[part], right.at[part], recv_r.at[part]).wait()
        return [
            jnp.concatenate(
                [right[part, 32 * j:32 * j + 32, kc].reshape(256, 128) for j in range(2)], axis=1
            )
            for kc in range(3)
        ]

    def multiply(channel, factors):
        return sum(
            jnp.dot(turned[channel, :, 256 * kc:256 * kc + 256], factors[kc],
                    preferred_element_type=f32)
            for kc in range(3)
        )

    def keep(part, j, t):
        sent_t[part, 32 * j:32 * j + 32] = t.reshape(32, 3, 8, 128).astype(bf16)

    def send_part(part):
        send(lambda chip: sent_t.at[part, chip], got_t.at[part, me], send_t.at[part],
             recv_t.at[part])

    factors = factor(0)
    t = multiply(0, factors)
    for j in range(2):
        keep(0, j, t[:, 128 * j:128 * j + 128])
    send_part(0)

    factors = factor(1)
    t0 = multiply(0, factors)
    t1 = multiply(1, factors)
    lane768 = lax.broadcasted_iota(jnp.int32, (768, 128), 1)
    for j in range(2):
        lanes = slice(128 * j, 128 * j + 128)
        keep(1, j, jnp.where(lane768 < 64, t0[:, lanes], t1[:, lanes]))
    send_part(1)

    factors = factor(2)
    t = multiply(1, factors)
    for j in range(2):
        keep(2, j, t[:, 128 * j:128 * j + 128])

    def send_last(it, carry):
        send(lambda chip: sent_t.at[2, chip, it], got_t.at[2, me, it], send_t.at[2],
             recv_last.at[it], FAR_FIRST)
        return carry

    lax.fori_loop(0, 3, send_last, 0)

    for part in range(2):
        pltpu.make_async_copy(sent_t.at[part], got_t.at[part], recv_t.at[part]).wait()

    def mixed(part, i):
        return mixing[part, pl.ds(i, 64, stride=8), :] * scale[part] + shift[part]

    def mean_of(values):
        total = jnp.sum(values, axis=0)
        return (total + pltpu.roll(total, 64, 1)) * (1.0 / 128)

    def finish_middle(it, carry):
        t = got_t[1, :, it].astype(f32)
        t = t - mean_of(t)[None]
        mixing[1] = (t * lax.rsqrt(mean_of(t * t) + epsilon)[None]).reshape(512, 128)
        w = wo_ref[...]
        for pair in range(4):
            even, odd = mixed(1, 2 * pair), mixed(1, 2 * pair + 1)
            top = jnp.where(lane64 < 64, even, pltpu.roll(odd, 64, 1))
            low = jnp.where(lane64 < 64, pltpu.roll(even, 64, 1), odd)
            both = jnp.concatenate([top, low], axis=0).astype(bf16)
            result = lax.dot_general(both, w, TN, preferred_element_type=f32)
            for n in range(2):
                k = 8 * it + 2 * pair + n
                out_ref[k, 128:192] = (gate[k, 128:192] * result[64 * n:64 * n + 64]).astype(bf16)
        return carry

    lax.fori_loop(0, 3, finish_middle, 0)

    def finish_ends(it, carry):
        pltpu.make_async_copy(sent_t.at[2, :, it], got_t.at[2, :, it], recv_last.at[it]).wait()
        t0, t2 = [got_t[part, :, it].astype(f32) for part in (0, 2)]
        mean = (jnp.sum(t0 + t2, axis=0) * (1.0 / 128))[None]
        t0 = t0 - mean
        t2 = t2 - mean
        root = lax.rsqrt(jnp.sum(t0 * t0 + t2 * t2, axis=0) * (1.0 / 128) + epsilon)[None]
        mixing[0] = (t0 * root).reshape(512, 128)
        mixing[2] = (t2 * root).reshape(512, 128)
        w = wo_ref[...]
        for i in range(8):
            ends = jnp.concatenate([mixed(0, i), mixed(2, i)], axis=0).astype(bf16)
            result = lax.dot_general(ends, w, TN, preferred_element_type=f32)
            k = 8 * it + i
            out_ref[k, 0:128] = (gate[k, 0:128] * result).astype(bf16)
        return carry

    lax.fori_loop(0, 3, finish_ends, 0)

    most = pl.ds(0, CHIPS - 1)
    pltpu.make_async_copy(sent_l.at[most], own.at[most], send_l).wait()
    for part in range(3):
        pltpu.make_async_copy(sent_r.at[part, most], right.at[part, most], send_r.at[part]).wait()
        pltpu.make_async_copy(sent_t.at[part, most], got_t.at[part, most], send_t.at[part]).wait()


def on_device(pair, ln_in_gain, ln_in_bias, w_proj, w_gate, ln_out_gain, ln_out_bias, w_out):
    dma = pltpu.SemaphoreType.DMA
    vmem = pl.BlockSpec(memory_space=pltpu.VMEM)
    return pl.pallas_call(
        kernel,
        name="triangle",
        out_shape=pltpu.VMEM((24, 192, 128), bf16),
        in_specs=[pl.BlockSpec(memory_space=pl.ANY)] * 8,
        out_specs=vmem,
        scratch_shapes=[
            pltpu.VMEM((24, 192, 128), bf16),
            pltpu.VMEM((1, 128), f32),
            pltpu.VMEM((1, 128), f32),
            pltpu.VMEM((128, 512), bf16),
            pltpu.VMEM((128, 128), bf16),
            pltpu.VMEM((1, 128), f32),
            pltpu.VMEM((1, 128), f32),
            pltpu.VMEM((128, 128), bf16),
            pltpu.VMEM((2, 256, 128), bf16),
            pltpu.VMEM((2, 128, 256), bf16),
            pltpu.VMEM((24, 192, 128), bf16),
            pltpu.VMEM((24, 192, 128), f32),
            pltpu.VMEM((3, 512, 128), f32),
            pltpu.VMEM((CHIPS, 3, 8, 384), bf16),
            pltpu.VMEM((3, CHIPS, 3, 8, 128), bf16),
            pltpu.VMEM((CHIPS, 3, 8, 384), bf16),
            pltpu.VMEM((CHIPS, 3, 8, 384), bf16),
            pltpu.VMEM((3, CHIPS, 3, 8, 128), bf16),
            pltpu.VMEM((2, 768, 768), bf16),
            pltpu.VMEM((3, CHIPS, 3, 8, 128), bf16),
            pltpu.VMEM((3, CHIPS, 3, 8, 128), bf16),
            pltpu.VMEM((3, 64, 128), f32),
            pltpu.VMEM((3, 64, 128), f32),
            pltpu.VMEM((3, 512, 128), f32),
            dma((7,)), dma((3,)), dma, dma((3,)), dma((3,)), dma((3,)), dma((3,)), dma((3,)), dma((3,)), dma((3,)), dma((3,)),
        ],
        compiler_params=pltpu.CompilerParams(collective_id=0, has_side_effects=True),
    )(pair, ln_in_gain.reshape(1, 128), ln_in_bias.reshape(1, 128), w_proj, w_gate,
      ln_out_gain.reshape(1, 128), ln_out_bias.reshape(1, 128), w_out)


def solution(mesh):
    return jax.shard_map(
        on_device,
        mesh=mesh,
        in_specs=(P("row", "loop", None), P(), P(), P(), P(), P(), P(), P()),
        out_specs=P("row", "loop", None),
        check_vma=False,
    )
```

```python
import jax
import jax.numpy as jnp
from jax import lax
from jax.experimental import pallas as pl
from jax.experimental.pallas import tpu as pltpu
from jax.sharding import PartitionSpec as P

epsilon = 1e-05
MESH = pl.DeviceIdType.MESH
f32 = jnp.float32
bf16 = jnp.bfloat16
CHIPS = 64
NT = (((1,), (1,)), ((), ()))
TN = (((0,), (0,)), ((), ()))


def distance(o):
    return sum(min(d, 4 - d) for d in (o // 16, o // 4 % 4, o % 4))


FAR_FIRST = sorted(range(1, CHIPS), key=lambda o: (-distance(o), o * 21 % CHIPS))
MIXED = [o * 21 % CHIPS for o in range(1, CHIPS)]


def normalize(values, gain, bias):
    center = values - jnp.mean(values, axis=-1, keepdims=True)
    spread = jnp.mean(center * center, axis=-1, keepdims=True)
    return center * lax.rsqrt(spread + epsilon) * gain + bias


def kernel(pair_hbm, gain_hbm, bias_hbm, w_hbm, wg_hbm, out_gain_hbm, out_bias_hbm, wo_hbm, out_ref,
           pair_ref, gain_ref, bias_ref, w_ref, wg_ref, out_gain_ref, out_bias_ref, wo_ref,
           wide, tall, normed, gate, major, sent_l, sent_r, own, other, right, turned, sent_t, got_t,
           scale, shift, mixing, half_mean, half_spread,
           load, load_pair, send_l, recv_l, pass_send, pass_recv, send_r, recv_r, send_t, recv_t, recv_last):
    def rows_of(kc):
        rows = pl.ds(pl.multiple_of(kc * 8, 8), 8)
        return pltpu.make_async_copy(pair_hbm.at[rows], pair_ref.at[rows], load_pair.at[kc])

    loads = [
        pltpu.make_async_copy(src, dst, load.at[n])
        for n, (src, dst) in enumerate((
            (w_hbm, w_ref), (gain_hbm, gain_ref), (bias_hbm, bias_ref), (wg_hbm, wg_ref),
            (out_gain_hbm, out_gain_ref), (out_bias_hbm, out_bias_ref), (wo_hbm, wo_ref),
        ))
    ]
    loads[0].start()
    for kc in range(3):
        rows_of(kc).start()
    for copy in loads[1:]:
        copy.start()

    row = lax.axis_index("row")
    loop = lax.axis_index("loop")
    core = loop % 2
    y_hi = loop // 2
    x = row // 8
    z = (row // 2) % 4
    y = y_hi * 2 + row % 2
    me = y_hi * 32 + row
    twin = (row, y_hi * 2 + (1 - core))
    xs = [((x + d) % 4) * 8 for d in range(4)]
    zs = [((z + d) % 4) * 2 for d in range(4)]
    ys = [(y + d) % 4 for d in range(4)]
    y_his = [v // 2 for v in ys]
    y_los = [v % 2 for v in ys]

    def each_peer(act, order):
        for o in order:
            dy = o // 4 % 4
            t_row = xs[o // 16] + zs[o % 4] + y_los[dy]
            act(y_his[dy] * 32 + t_row, (t_row, y_his[dy] * 2 + core))

    def send(src, dst, send_sem, recv_sem, order=MIXED):
        def act(chip, device):
            pltpu.make_async_remote_copy(
                src(chip), dst, send_sem, recv_sem, device_id=device, device_id_type=MESH
            ).start()

        each_peer(act, order)
        pltpu.make_async_copy(src(me), dst, recv_sem).start()

    barrier = pltpu.get_barrier_semaphore()
    each_peer(lambda chip, device: pl.semaphore_signal(
        barrier, inc=1, device_id=device, device_id_type=MESH), FAR_FIRST)
    pl.semaphore_signal(barrier, inc=1, device_id=twin, device_id_type=MESH)

    def flip(side):
        flipped = w_ref[:, 256 * side:256 * side + 256].astype(f32).T.astype(bf16)
        wide[side] = flipped
        for kind in range(2):
            for half in range(2):
                at = 128 * kind + 64 * half
                tall[side, pl.ds(64 * kind, 64), pl.ds(128 * half, 128)] = flipped[at:at + 64]

    for copy in loads[0:3]:
        copy.wait()
    flip(0)

    def project(side, kc):
        for k in range(8):
            values = normed[8 * kc + k]
            head = values[0:128]
            rest = values[128:192]
            zero = jnp.zeros_like(rest)
            both = jnp.concatenate(
                [jnp.concatenate([rest, zero], axis=1), jnp.concatenate([zero, rest], axis=1)],
                axis=0,
            )
            a = lax.dot_general(wide[side], head, NT, preferred_element_type=f32)
            b = lax.dot_general(tall[side], both, NT, preferred_element_type=f32)
            rows = pl.ds(64 * k, 64)
            ends = jax.nn.sigmoid(a[0:128]) * a[128:256]
            major[0, rows] = ends[0:64]
            major[1, rows] = jax.nn.sigmoid(b[0:64]) * b[64:128]
            major[2, rows] = ends[64:128]

    def column(part, c):
        return major[part, pl.ds(c, 8, stride=64), :].astype(bf16)

    def project_left(kc):
        rows_of(kc).wait()
        for k in range(8):
            values = pair_ref[8 * kc + k].astype(f32)
            normed[8 * kc + k] = normalize(values, gain_ref[...], bias_ref[...]).astype(bf16)
        project(0, kc)
        for c in range(CHIPS):
            for part in range(3):
                sent_l[c, kc, :, pl.ds(128 * part, 128)] = column(part, c)

    def send_left(kc):
        send(lambda chip: sent_l.at[chip, kc], own.at[me, kc], send_l, recv_l.at[kc])

    project_left(0)
    pl.semaphore_wait(barrier, CHIPS)
    send_left(0)

    def rest_of_left(kc, carry):
        project_left(kc)
        send_left(kc)
        return carry

    lax.fori_loop(1, 3, rest_of_left, 0)

    flip(1)

    def project_right(kc, carry):
        project(1, kc)
        for c in range(CHIPS):
            for part in range(3):
                sent_r[part, c, kc] = column(part, c)
        return carry

    lax.fori_loop(0, 3, project_right, 0)

    def send_right(part, carry):
        send(lambda chip: sent_r.at[part, chip], right.at[part, me], send_r.at[part],
             recv_r.at[part])
        return carry

    for copy in loads[3:]:
        copy.wait()

    def open_gate(k, carry):
        gate[k] = jax.nn.sigmoid(jnp.dot(normed[k], wg_ref[...], preferred_element_type=f32))
        return carry

    def open_gates():
        lax.fori_loop(0, 24, open_gate, 0)

    pl.when(core == 1)(open_gates)
    lax.fori_loop(0, 3, send_right, 0)
    pl.when(core == 0)(open_gates)


    diagonal = (lax.broadcasted_iota(jnp.int32, (128, 128), 0)
                == lax.broadcasted_iota(jnp.int32, (128, 128), 1))
    lane64 = lax.broadcasted_iota(jnp.int32, (64, 128), 1)
    for source, dest in ((out_gain_ref, scale), (out_bias_ref, shift)):
        one = jnp.sum(jnp.where(diagonal, source[...], 0.0), axis=1, keepdims=True)
        spread_out = jnp.broadcast_to(one, (128, 128))
        dest[0] = spread_out[0:64]
        dest[1] = jnp.where(lane64 < 64, spread_out[0:64], spread_out[64:128])
        dest[2] = spread_out[64:128]

    def turn(ref, kc, of):
        def block(h, carry):
            t = ref[pl.ds(h * 32, 32), kc].reshape(256, 384).T
            first = (h * 2 + of) * 192
            lanes = pl.ds(pl.multiple_of(kc * 256, 256), 256)
            turned[0, pl.ds(pl.multiple_of(first, 64), 192), lanes] = t[0:192]
            turned[1, pl.ds(pl.multiple_of(first + 128, 64), 64), lanes] = t[192:256]
            turned[1, pl.ds(pl.multiple_of(first, 64), 128), lanes] = t[256:384]
            return carry

        lax.fori_loop(0, 2, block, 0)

    def take_left(kc, carry):
        pltpu.make_async_copy(own.at[:, kc], own.at[:, kc], recv_l.at[kc]).wait()
        passing = pltpu.make_async_remote_copy(
            own.at[:, kc], other.at[:, kc], pass_send.at[kc], pass_recv.at[kc],
            device_id=twin, device_id_type=MESH,
        )
        passing.start()
        turn(own, kc, core)
        passing.wait()
        turn(other, kc, 1 - core)
        return carry

    lax.fori_loop(0, 3, take_left, 0)

    def factor(part):
        pltpu.make_async_copy(sent_r.at[part], right.at[part], recv_r.at[part]).wait()
        return [
            jnp.concatenate(
                [right[part, 32 * j:32 * j + 32, kc].reshape(256, 128) for j in range(2)], axis=1
            )
            for kc in range(3)
        ]

    def multiply(channel, factors):
        return sum(
            jnp.dot(turned[channel, :, 256 * kc:256 * kc + 256], factors[kc],
                    preferred_element_type=f32)
            for kc in range(3)
        )

    def keep(part, j, t):
        sent_t[part, 32 * j:32 * j + 32] = t.reshape(32, 3, 8, 128).astype(bf16)

    def send_part(part):
        send(lambda chip: sent_t.at[part, chip], got_t.at[part, me], send_t.at[part],
             recv_t.at[part])

    factors = factor(0)
    t = multiply(0, factors)
    for j in range(2):
        keep(0, j, t[:, 128 * j:128 * j + 128])
    send_part(0)

    factors = factor(1)
    t0 = multiply(0, factors)
    t1 = multiply(1, factors)
    lane768 = lax.broadcasted_iota(jnp.int32, (768, 128), 1)
    for j in range(2):
        lanes = slice(128 * j, 128 * j + 128)
        keep(1, j, jnp.where(lane768 < 64, t0[:, lanes], t1[:, lanes]))
    send_part(1)

    factors = factor(2)
    t = multiply(1, factors)
    for j in range(2):
        keep(2, j, t[:, 128 * j:128 * j + 128])

    def send_last(it, carry):
        send(lambda chip: sent_t.at[2, chip, it], got_t.at[2, me, it], send_t.at[2],
             recv_last.at[it], FAR_FIRST)
        return carry

    lax.fori_loop(0, 3, send_last, 0)

    for part in range(2):
        pltpu.make_async_copy(sent_t.at[part], got_t.at[part], recv_t.at[part]).wait()

    def mixed(part, i):
        return mixing[part, pl.ds(i, 64, stride=8), :] * scale[part] + shift[part]

    def mean_of(values):
        total = jnp.sum(values, axis=0)
        return (total + pltpu.roll(total, 64, 1)) * (1.0 / 128)

    def finish_middle(it, carry):
        t = got_t[1, :, it].astype(f32)
        t = t - mean_of(t)[None]
        mixing[1] = (t * lax.rsqrt(mean_of(t * t) + epsilon)[None]).reshape(512, 128)
        w = wo_ref[...]
        for pair in range(4):
            even, odd = mixed(1, 2 * pair), mixed(1, 2 * pair + 1)
            top = jnp.where(lane64 < 64, even, pltpu.roll(odd, 64, 1))
            low = jnp.where(lane64 < 64, pltpu.roll(even, 64, 1), odd)
            both = jnp.concatenate([top, low], axis=0).astype(bf16)
            result = lax.dot_general(both, w, TN, preferred_element_type=f32)
            for n in range(2):
                k = 8 * it + 2 * pair + n
                out_ref[k, 128:192] = (gate[k, 128:192] * result[64 * n:64 * n + 64]).astype(bf16)
        t0 = got_t[0, :, it].astype(f32)
        mean = jnp.sum(t0, axis=0) * (1.0 / 64)
        t0 = t0 - mean[None]
        half_mean[it] = mean
        half_spread[it] = jnp.sum(t0 * t0, axis=0)
        return carry

    lax.fori_loop(0, 3, finish_middle, 0)

    def finish_ends(it, carry):
        pltpu.make_async_copy(sent_t.at[2, :, it], got_t.at[2, :, it], recv_last.at[it]).wait()
        t0, t2 = [got_t[part, :, it].astype(f32) for part in (0, 2)]
        low = half_mean[it]
        high = jnp.sum(t2, axis=0) * (1.0 / 64)
        apart = t2 - high[None]
        spread = half_spread[it] + jnp.sum(apart * apart, axis=0)
        spread = (spread + (high - low) * (high - low) * 32.0) * (1.0 / 128)
        root = lax.rsqrt(spread + epsilon)[None]
        mean = ((low + high) * 0.5)[None]
        t0 = t0 - mean
        t2 = t2 - mean
        mixing[0] = (t0 * root).reshape(512, 128)
        mixing[2] = (t2 * root).reshape(512, 128)
        w = wo_ref[...]
        for i in range(8):
            ends = jnp.concatenate([mixed(0, i), mixed(2, i)], axis=0).astype(bf16)
            result = lax.dot_general(ends, w, TN, preferred_element_type=f32)
            k = 8 * it + i
            out_ref[k, 0:128] = (gate[k, 0:128] * result).astype(bf16)
        return carry

    lax.fori_loop(0, 3, finish_ends, 0)

    most = pl.ds(0, CHIPS - 1)
    pltpu.make_async_copy(sent_l.at[most], own.at[most], send_l).wait()
    for part in range(3):
        pltpu.make_async_copy(sent_r.at[part, most], right.at[part, most], send_r.at[part]).wait()
        pltpu.make_async_copy(sent_t.at[part, most], got_t.at[part, most], send_t.at[part]).wait()


def on_device(pair, ln_in_gain, ln_in_bias, w_proj, w_gate, ln_out_gain, ln_out_bias, w_out):
    dma = pltpu.SemaphoreType.DMA
    vmem = pl.BlockSpec(memory_space=pltpu.VMEM)
    return pl.pallas_call(
        kernel,
        name="triangle",
        out_shape=pltpu.VMEM((24, 192, 128), bf16),
        in_specs=[pl.BlockSpec(memory_space=pl.ANY)] * 8,
        out_specs=vmem,
        scratch_shapes=[
            pltpu.VMEM((24, 192, 128), bf16),
            pltpu.VMEM((1, 128), f32),
            pltpu.VMEM((1, 128), f32),
            pltpu.VMEM((128, 512), bf16),
            pltpu.VMEM((128, 128), bf16),
            pltpu.VMEM((1, 128), f32),
            pltpu.VMEM((1, 128), f32),
            pltpu.VMEM((128, 128), bf16),
            pltpu.VMEM((2, 256, 128), bf16),
            pltpu.VMEM((2, 128, 256), bf16),
            pltpu.VMEM((24, 192, 128), bf16),
            pltpu.VMEM((24, 192, 128), f32),
            pltpu.VMEM((3, 512, 128), f32),
            pltpu.VMEM((CHIPS, 3, 8, 384), bf16),
            pltpu.VMEM((3, CHIPS, 3, 8, 128), bf16),
            pltpu.VMEM((CHIPS, 3, 8, 384), bf16),
            pltpu.VMEM((CHIPS, 3, 8, 384), bf16),
            pltpu.VMEM((3, CHIPS, 3, 8, 128), bf16),
            pltpu.VMEM((2, 768, 768), bf16),
            pltpu.VMEM((3, CHIPS, 3, 8, 128), bf16),
            pltpu.VMEM((3, CHIPS, 3, 8, 128), bf16),
            pltpu.VMEM((3, 64, 128), f32),
            pltpu.VMEM((3, 64, 128), f32),
            pltpu.VMEM((3, 512, 128), f32),
            pltpu.VMEM((3, 8, 128), f32),
            pltpu.VMEM((3, 8, 128), f32),
            dma((7,)), dma((3,)), dma, dma((3,)), dma((3,)), dma((3,)), dma((3,)), dma((3,)), dma((3,)), dma((3,)), dma((3,)),
        ],
        compiler_params=pltpu.CompilerParams(collective_id=0, has_side_effects=True),
    )(pair, ln_in_gain.reshape(1, 128), ln_in_bias.reshape(1, 128), w_proj, w_gate,
      ln_out_gain.reshape(1, 128), ln_out_bias.reshape(1, 128), w_out)


def solution(mesh):
    return jax.shard_map(
        on_device,
        mesh=mesh,
        in_specs=(P("row", "loop", None), P(), P(), P(), P(), P(), P(), P()),
        out_specs=P("row", "loop", None),
        check_vma=False,
    )
```
